256 devices in a mesh: kgrp: 16 (over y, z_hi, core), wrow: 16 (over z_lo, x).
Axes of the slice: x: 4, y: 4, z: 8 (z_hi: 2, z_lo: 4; z = z_hi * 4 + z_lo), core: 2. Of those that a mesh axis runs over, the one named last changes fastest.
Arguments:
- orbitals: bfloat16 [16, 1024, 384], P('kgrp', 'wrow'), may hold values from -0.71875 to 0.71875
- energies: float32 [16, 192], replicated, may hold values from -2 to 2
- perm_table: int32 [64, 16], replicated, may hold values from 0 to 15, each once within a row
- momenta: int32 [2], replicated, may hold values from 0 to 63
- screened_w: bfloat16 [2, 2, 16, 1024, 1024], P(None, None, None, 'wrow'), may hold values from -6 to 6
Outputs:
- sigma: float32 [16, 16, 192, 384], P('kgrp', None, 'wrow')
The draws below stay inside these ranges and needn't reach their ends.
Inputs may be any that keep to these rules, and one draw needn't show every extreme that they name: `perm_table`: each row is a permutation of the 16 k-points: entry k names the k-point k minus that row's momentum transfer. `momenta`: each entry names a row of perm_table; the two may coincide.
All inputs are finite; a program needn't handle non-finite values.
Results may differ from the reference program's by a relative error of at most 0.0055.
Values may be sent and summed in bfloat16 or wider, within the bound.
A program may use at most 128 MiB of HBM per device.

```python
import jax
import jax.numpy as jnp
from jax import lax

NPTS = 1024
NORB = 192
NTAU = 16
NQ = 2
NQTAB = 64
NK = 16


def shard_levels(own_key, extent, split, least, high):
    factor_of = 1.0
    for position, blocks in split:
        draws = jax.random.uniform(jax.random.fold_in(jax.random.fold_in(own_key, 6), position), (blocks,), jnp.float32, least / len(split), high / len(split))
        factor_of = factor_of * jnp.repeat(jnp.exp(draws), extent[position] // blocks).reshape((-1,) + (1,) * (len(extent) - 1 - position))
    return factor_of


def centred(rng, dims, width, reach, pieces=(), kind=jnp.bfloat16):
    values = jax.random.normal(rng, dims, jnp.float32) * width
    if len(pieces) > 0:
        values = shard_levels(rng, dims, pieces, -0.22, 0.18) * values
    return jnp.clip(values, min=-reach, max=reach).astype(kind)


def setup_inputs(seed: int = 0) -> dict:
    streams_of = jax.random.split(jax.random.key(seed), 6)
    return {
        "orbitals": centred(streams_of[0], (NK, NPTS, 2 * NORB), 0.12, 0.71875, ((0, 16), (1, 16))),
        "energies": jnp.clip(jax.random.uniform(streams_of[1], (NK, NORB), jnp.float32, -2.0, 2.0), -2.0, 2.0),
        "perm_table": jax.vmap(lambda own: jax.random.permutation(own, NK))(jax.random.split(streams_of[2], NQTAB)).reshape((NQTAB, NK)).astype(jnp.int32),
        "momenta": jax.random.randint(streams_of[3], (NQ,), 0, NQTAB).astype(jnp.int32),
        "screened_w": centred(streams_of[4], (NQ, 2, NTAU, NPTS, NPTS), 1.0, 6.0, ((3, 16),)),
    }


BETA = 8.0


def occupation(energy_row, tau_count):
    tau_grid = BETA * (jnp.arange(tau_count, dtype=jnp.float32) + 0.5) / tau_count
    return -jnp.exp(-tau_grid[:, None] * energy_row[None, :] - jax.nn.softplus(-BETA * energy_row)[None, :])


def rotate(matrix):
    middle = matrix.shape[-1] // 2
    return jnp.concatenate([-matrix[..., middle:], matrix[..., :middle]], axis=-1)


def scaled_rows(point_rows, factor):
    doubled = jnp.concatenate([factor, factor], axis=1)
    return (point_rows.astype(jnp.float32)[None] * doubled[:, None, :]).astype(jnp.bfloat16)


def project(own_rows, half_proj):
    orbital_count = own_rows.shape[1] // 2
    blocks = jnp.einsum('pi,tpj->tij', own_rows.astype(jnp.float32), half_proj.astype(jnp.float32))
    real_part = blocks[:, :orbital_count, :orbital_count] + blocks[:, orbital_count:, orbital_count:]
    imag_part = blocks[:, :orbital_count, orbital_count:] - blocks[:, orbital_count:, :orbital_count]
    return jnp.concatenate([real_part, imag_part], axis=2)


def reference(orbitals, energies, perm_table, momenta, screened_w):
    def one_k(k_point):
        own_orbitals = orbitals[k_point]
        sigma_sum = jnp.zeros((NTAU, NORB, 2 * NORB), jnp.float32)
        for q_slot in range(NQ):
            source = perm_table[momenta[q_slot], k_point]
            partner = orbitals[source]
            factor = occupation(energies[source], NTAU)
            flat_left = scaled_rows(partner, factor).reshape(-1, 2 * NORB)
            green_real = jnp.dot(flat_left, partner.T, preferred_element_type=jnp.float32)
            green_imag = jnp.dot(flat_left, rotate(partner).T, preferred_element_type=jnp.float32)
            w_slice = screened_w[q_slot].reshape(2, NTAU * NPTS, NPTS).astype(jnp.float32)
            screen_real = (green_real * w_slice[0] - green_imag * w_slice[1]).astype(jnp.bfloat16)
            screen_imag = (green_real * w_slice[1] + green_imag * w_slice[0]).astype(jnp.bfloat16)
            half_proj = (jnp.dot(screen_real, own_orbitals, preferred_element_type=jnp.float32)
                         + jnp.dot(screen_imag, rotate(own_orbitals), preferred_element_type=jnp.float32)).astype(jnp.bfloat16)
            sigma_sum = sigma_sum + project(own_orbitals, half_proj.reshape(NTAU, NPTS, 2 * NORB))
        return sigma_sum

    return lax.map(one_k, jnp.arange(NK, dtype=jnp.int32))
```

```python
import functools

import jax
import jax.numpy as jnp
from jax import lax
from jax.experimental import pallas as pl
from jax.experimental.pallas import tpu as pltpu
from jax.sharding import PartitionSpec as P

BETA = 8.0
MESH = pl.DeviceIdType.MESH
NT = (((1,), (1,)), ((), ()))
NN = (((1,), (0,)), ((), ()))


def sign_row(width, first, second):
    half = width // 2
    lane = lax.broadcasted_iota(jnp.int32, (1, width), 1)
    return jnp.where(lane < half, first, second).astype(jnp.float32)


def swap_halves(x):
    half = x.shape[1] // 2
    return jnp.concatenate([x[:, half:], x[:, :half]], axis=1)


def kernel(perm_ref, mom_ref, energy_ref, orb_ref, w_hbm, out_ref,
           xs, kg, wv, scr, lsc, hsend, hrecv, xkt, order, occ,
           rsend, rrecv, fsend, frecv,
           gsend, grecv, ksend, krecv, kcore, hss, hrs, rss, rrs, fss, frs, wsem, osem):
    g = lax.axis_index("kgrp")
    w = lax.axis_index("wrow")
    y, h, c = lax.div(g, 4), lax.rem(lax.div(g, 2), 2), lax.rem(g, 2)
    z, x = lax.div(w, 4), lax.rem(w, 4)
    rows, width = xs.shape[2], xs.shape[3]
    taus = wv.shape[2]

    def wrap(v):
        return lax.rem(v, 4)

    def kdev(y_, h_, c_):
        return y_ * 4 + h_ * 2 + c_

    def wdev(z_, x_):
        return z_ * 4 + x_

    own_x = pltpu.make_async_copy(orb_ref.at[0], xs.at[0, w], osem.at[0])
    own_k = pltpu.make_async_copy(orb_ref.at[0], kg.at[g], osem.at[1])
    own_x.start()
    own_k.start()

    barrier = pltpu.get_barrier_semaphore()
    partner = kdev(y, h, 1 - c)
    across = kdev(y, 1 - h, c)
    up, down = kdev(wrap(y + 1), h, c), kdev(wrap(y + 3), h, c)
    beyond = kdev(wrap(y + 2), h, c)
    for peer in (across, up, down, beyond, partner):
        pl.semaphore_signal(barrier, inc=1, device_id=(peer, w), device_id_type=MESH)
    for d in (2, 1, 3):
        pl.semaphore_signal(barrier, inc=1, device_id=(g, wdev(wrap(z + d), x)), device_id_type=MESH)
        pl.semaphore_signal(barrier, inc=1, device_id=(g, wdev(z, wrap(x + d))), device_id_type=MESH)
    own_x.wait()
    own_k.wait()
    pl.semaphore_wait(barrier, 11)

    def kcopy(block, peer):
        return pltpu.make_async_remote_copy(
            src_ref=kg.at[block], dst_ref=kg.at[block], send_sem=ksend.at[0],
            recv_sem=krecv.at[block], device_id=(peer, w), device_id_type=MESH)

    def kpass(block):
        pltpu.make_async_remote_copy(
            src_ref=kg.at[block], dst_ref=kg.at[block], send_sem=ksend.at[0],
            recv_sem=kcore.at[0], device_id=(partner, w), device_id_type=MESH).start()

    def kwait(block):
        kcopy(block, across).wait_recv()

    def gcopy(s, block, peer):
        return pltpu.make_async_remote_copy(
            src_ref=xs.at[s, block], dst_ref=xs.at[s, block], send_sem=gsend.at[s],
            recv_sem=grecv.at[s, block], device_id=(g, peer), device_id_type=MESH)

    left, right = wdev(z, wrap(x + 3)), wdev(z, wrap(x + 1))

    def gwait(s, block):
        gcopy(s, block, right).wait_recv()

    def gstart_z(s):
        gcopy(s, w, wdev(wrap(z + 1), x)).start()
        gcopy(s, w, wdev(wrap(z + 3), x)).start()
        gcopy(s, w, wdev(wrap(z + 2), x)).start()

    def gstart_x(s):
        gcopy(s, w, right).start()
        gcopy(s, w, left).start()

    def gforward(s, d):
        block = wdev(wrap(z + d), x)
        gwait(s, block)
        gcopy(s, block, right).start()
        gcopy(s, block, left).start()

    def grelay(s, d):
        if d < 2:
            block, peer = wdev(wrap(z + d), wrap(x + 3)), right
        else:
            block, peer = wdev(wrap(z + d), wrap(x + 1)), left
        gwait(s, block)
        gcopy(s, block, peer).start()

    def gfinish(s, d):
        gwait(s, wdev(wrap(z + d), wrap(x + (1 if d < 2 else 3))))
        gwait(s, wdev(wrap(z + d), wrap(x + 2)))

    def kspread(block):
        for peer in (beyond, up, down):
            kcopy(block, peer).start()

    def ktake(yy, hh):
        block = kdev(wrap(y + yy), hh, c)
        kwait(block)
        kpass(block)

    kcopy(g, across).start()
    kspread(g)
    gstart_x(0)
    kpass(g)
    for i in range(4):
        pltpu.make_async_copy(w_hbm.at[i // 2, i % 2], wv.at[i // 2, i % 2], wsem.at[i]).start()
    ktake(1, h)
    gstart_z(0)
    ktake(3, h)
    ktake(2, h)
    grelay(0, 0)
    row = lax.broadcasted_iota(jnp.int32, (192, 192), 0)
    col = lax.broadcasted_iota(jnp.int32, (192, 192), 1)
    part, inner = lax.div(row, 48), lax.rem(row, 48)
    split = lax.div(inner, 12) * 48 + part * 12 + lax.rem(inner, 12)
    tau_row = lax.rem(row, 16)
    merge = lax.rem(tau_row, 4) * 48 + lax.div(tau_row, 4) * 12 + lax.div(row, 16)
    order[0] = jnp.where(col == split, 1.0, 0.0).astype(jnp.bfloat16)
    order[1] = jnp.where(col == merge, 1.0, 0.0).astype(jnp.bfloat16)
    own_row = perm_ref[pl.ds(g, 1), :]
    lane = lax.broadcasted_iota(jnp.int32, own_row.shape, 1)
    sources = [jnp.sum(jnp.where(lane == mom_ref[q], own_row, 0)) for q in range(2)]
    gfinish(0, 0)
    row = lax.broadcasted_iota(jnp.int32, (width, width), 0)
    col = lax.broadcasted_iota(jnp.int32, (width, width), 1)
    pick = jnp.where(row == col, 1.0, 0.0).astype(jnp.bfloat16)
    strip = xs[0, pl.ds(z * 4, 4)].reshape(4 * rows, width)
    xkt[...] = lax.dot_general(pick, strip, NT, preferred_element_type=jnp.float32).astype(jnp.bfloat16)
    mine = kdev(y, 1 - h, c)
    kwait(mine)
    kspread(mine)
    kpass(mine)
    gforward(0, 1)
    gforward(0, 3)
    gforward(0, 2)
    ktake(1, 1 - h)
    ktake(3, 1 - h)
    ktake(2, 1 - h)
    grelay(0, 1)
    grelay(0, 3)
    pltpu.make_async_remote_copy(
        src_ref=kg.at[pl.ds(0, 8)], dst_ref=kg.at[pl.ds(0, 8)], send_sem=ksend.at[0],
        recv_sem=kcore.at[0], device_id=(partner, w), device_id_type=MESH).wait_recv()

    for q in range(2):
        xs[1 + q, w] = kg[sources[q]]
    for s in (1, 2):
        gstart_z(s)
        gstart_x(s)

    minus_plus = sign_row(width, -1.0, 1.0)
    plus_minus = sign_row(width, 1.0, -1.0)
    tau = (lax.broadcasted_iota(jnp.int32, (taus, 1), 0).astype(jnp.float32) + 0.5) * (BETA / taus)
    for q in range(2):
        energy = energy_ref[pl.ds(sources[q], 1), :]
        soft = -BETA * energy
        soft = jnp.maximum(soft, 0.0) + jnp.log(1.0 + jnp.exp(-jnp.abs(soft)))
        factor = -jnp.exp(-tau * energy - soft)
        occ[q] = jnp.concatenate([factor, factor], axis=1)

    def tau_of(r, e):
        return r * 4 + wrap(x + e)

    def left_rows(q, r):
        base = xs[1 + q, w].astype(jnp.float32)
        scaled = jnp.concatenate(
            [base * occ[q, pl.ds(tau_of(r, e), 1), :] for e in range(4)], axis=0)
        lsc[q, r, :256] = scaled.astype(jnp.bfloat16)
        lsc[q, r, 256:] = (swap_halves(scaled) * plus_minus).astype(jnp.bfloat16)

    def left_round(r, carry):
        left_rows(0, r)
        left_rows(1, r)
        return carry

    lax.fori_loop(0, 4, left_round, 0, unroll=True)
    grelay(0, 2)

    def screen(q, n, r):
        cols = pl.ds(pl.multiple_of(n * 256, 256), 256)
        tile = xs[1 + q, pl.ds(n * 4, 4)].reshape(256, width)
        green = lax.dot_general(lsc[q, r], tile, NT, preferred_element_type=jnp.float32)
        for e in range(4):
            t = tau_of(r, e)
            real_rows, imag_rows = slice(e * 64, e * 64 + 64), slice(256 + e * 64, 320 + e * 64)
            gr, gi = green[real_rows], green[imag_rows]
            wr = wv[q, 0, t, :, cols].astype(jnp.float32)
            wi = wv[q, 1, t, :, cols].astype(jnp.float32)
            sr = gr * wr - gi * wi
            si = gr * wi + gi * wr
            if q == 1:
                sr = sr + scr[r, real_rows, cols].astype(jnp.float32)
                si = si + scr[r, imag_rows, cols].astype(jnp.float32)
            scr[r, real_rows, cols] = sr.astype(jnp.bfloat16)
            scr[r, imag_rows, cols] = si.astype(jnp.bfloat16)

    def tile(q, d):
        n = wrap(z + d)

        def one_round(r, carry):
            screen(q, n, r)
            return carry

        lax.fori_loop(0, 4, one_round, 0, unroll=True)

    grelay(1, 0)
    gforward(1, 1)
    gforward(1, 3)
    gforward(1, 2)
    for d in (1, 3, 2):
        gfinish(0, d)
    for i in range(2):
        pltpu.make_async_copy(w_hbm.at[0, i], wv.at[0, i], wsem.at[i]).wait()
    gfinish(1, 0)
    tile(0, 0)
    grelay(1, 1)
    grelay(1, 3)
    gforward(2, 1)
    grelay(2, 0)
    gfinish(1, 1)
    tile(0, 1)
    gforward(2, 3)
    grelay(1, 2)
    gforward(2, 2)
    gfinish(1, 3)
    tile(0, 3)
    grelay(2, 1)
    grelay(2, 3)
    gfinish(1, 2)
    tile(0, 2)
    for i in range(2):
        pltpu.make_async_copy(w_hbm.at[1, i], wv.at[1, i], wsem.at[2 + i]).wait()
    gfinish(2, 0)
    tile(1, 0)
    grelay(2, 2)
    gfinish(2, 1)
    tile(1, 1)
    gfinish(2, 3)
    tile(1, 3)
    gfinish(2, 2)

    def hcopy(r, e):
        return pltpu.make_async_remote_copy(
            src_ref=hsend.at[r, e], dst_ref=hrecv.at[r, x], send_sem=hss.at[0],
            recv_sem=hrs.at[r], device_id=(g, wdev(z, wrap(x + e))), device_id_type=MESH)

    def last(r, carry):
        screen(1, wrap(z + 2), r)
        both = lax.dot_general(scr[r], xs[0].reshape(16 * rows, width), NN,
                               preferred_element_type=jnp.float32)
        half = both[:256] + swap_halves(both[256:]) * minus_plus
        half = half.astype(jnp.bfloat16)
        for e in (2, 1, 3):
            hsend[r, e] = half[e * 64:e * 64 + 64]
        hrecv[r, x] = half[:64]
        for e in (2, 1, 3):
            hcopy(r, e).start()
        return carry

    lax.fori_loop(0, 4, last, 0, unroll=True)

    def rcopy(r, d):
        other = wrap(z + d)
        return pltpu.make_async_remote_copy(
            src_ref=rsend.at[r, other], dst_ref=rrecv.at[r, z], send_sem=rss.at[0],
            recv_sem=rrs.at[0], device_id=(g, wdev(other, x)), device_id_type=MESH)

    def project(r):
        pltpu.make_async_remote_copy(
            src_ref=hrecv.at[r, pl.ds(0, 3)], dst_ref=hrecv.at[r, pl.ds(0, 3)], send_sem=hss.at[0],
            recv_sem=hrs.at[r], device_id=(g, right), device_id_type=MESH).wait_recv()
        total = lax.dot_general(xkt[...], hrecv[r].reshape(4 * rows, width), NN,
                                preferred_element_type=jnp.float32)
        sigma = total[:192] + swap_halves(total[192:]) * plus_minus
        sigma = sigma.reshape(4, 48, width)
        rsend[r] = sigma.astype(jnp.bfloat16)
        for d in (2, 1, 3):
            rcopy(r, d).start()

    for r in range(4):
        project(r)

    pltpu.make_async_remote_copy(
        src_ref=rrecv.at[pl.ds(0, 3)], dst_ref=rrecv.at[pl.ds(0, 3)], send_sem=rss.at[0],
        recv_sem=rrs.at[0], device_id=(g, right), device_id_type=MESH).wait_recv()
    sums = []
    for r in range(4):
        total = rsend[r, z].astype(jnp.float32)
        for d in range(1, 4):
            total = total + rrecv[r, wrap(z + d)].astype(jnp.float32)
        sums.append(total)
    summed = jnp.concatenate(sums, axis=0).astype(jnp.bfloat16)
    pieces = lax.dot_general(order[0], summed, NN, preferred_element_type=jnp.float32)
    fsend[...] = pieces.astype(jnp.bfloat16).reshape(4, 48, width)
    frecv[x] = fsend[x]
    for e in (2, 1, 3):
        other = wrap(x + e)
        pltpu.make_async_remote_copy(
            src_ref=fsend.at[other], dst_ref=frecv.at[x], send_sem=fss.at[0],
            recv_sem=frs.at[0], device_id=(g, wdev(z, other)), device_id_type=MESH).start()

    for s in range(3):
        pltpu.make_async_remote_copy(
            src_ref=xs.at[s, pl.ds(0, 15)], dst_ref=xs.at[s, pl.ds(0, 15)], send_sem=gsend.at[s],
            recv_sem=grecv.at[s, 0], device_id=(g, right), device_id_type=MESH).wait_send()
    pltpu.make_async_remote_copy(
        src_ref=kg.at[pl.ds(0, 15)], dst_ref=kg.at[pl.ds(0, 15)], send_sem=ksend.at[0],
        recv_sem=kcore.at[0], device_id=(partner, w), device_id_type=MESH).wait_send()
    pltpu.make_async_remote_copy(
        src_ref=hsend.at[pl.ds(0, 3)], dst_ref=hrecv.at[pl.ds(0, 3)], send_sem=hss.at[0],
        recv_sem=hrs.at[0], device_id=(g, right), device_id_type=MESH).wait_send()
    pltpu.make_async_remote_copy(
        src_ref=rsend.at[pl.ds(0, 3)], dst_ref=rrecv.at[pl.ds(0, 3)], send_sem=rss.at[0],
        recv_sem=rrs.at[0], device_id=(g, right), device_id_type=MESH).wait_send()
    pltpu.make_async_remote_copy(
        src_ref=fsend.at[pl.ds(0, 3)], dst_ref=frecv.at[pl.ds(0, 3)], send_sem=fss.at[0],
        recv_sem=frs.at[0], device_id=(g, right), device_id_type=MESH).wait()
    out_ref[0] = lax.dot_general(order[1], frecv[...].reshape(192, width), NN,
                                 preferred_element_type=jnp.float32).reshape(12, 16, width)


def shards(orbitals, energies, perm_table, momenta, screened_w):
    _, rows, width = orbitals.shape
    taus, points = screened_w.shape[2], screened_w.shape[4]
    bf16, f32 = jnp.bfloat16, jnp.float32
    dma = pltpu.SemaphoreType.DMA
    smem = pl.BlockSpec(memory_space=pltpu.SMEM)
    vmem = pl.BlockSpec(memory_space=pltpu.VMEM)
    sigma = pl.pallas_call(
        kernel,
        out_shape=jax.ShapeDtypeStruct((1, 12, taus, width), f32),
        in_specs=[vmem, smem, vmem, pl.BlockSpec(memory_space=pl.ANY), pl.BlockSpec(memory_space=pl.ANY)],
        out_specs=vmem,
        scratch_shapes=[
            pltpu.VMEM((3, 16, rows, width), bf16),
            pltpu.VMEM((16, rows, width), bf16),
            pltpu.VMEM((2, 2, taus, rows, points), bf16),
            pltpu.VMEM((4, 512, points), bf16),
            pltpu.VMEM((2, 4, 512, width), bf16),
            pltpu.VMEM((4, 4, rows, width), bf16),
            pltpu.VMEM((4, 4, rows, width), bf16),
            pltpu.VMEM((width, 4 * rows), bf16),
            pltpu.VMEM((2, 192, 192), bf16),
            pltpu.VMEM((2, taus, width), f32),
            pltpu.VMEM((4, 4, 48, width), bf16),
            pltpu.VMEM((4, 4, 48, width), bf16),
            pltpu.VMEM((4, 48, width), bf16),
            pltpu.VMEM((4, 48, width), bf16),
            dma((3,)), dma((3, 16)), dma((1,)), dma((16,)), dma((1,)),
            dma((1,)), dma((4,)), dma((1,)), dma((1,)), dma((1,)), dma((1,)),
            dma((4,)), dma((2,)),
        ],
        compiler_params=pltpu.CompilerParams(collective_id=0, has_side_effects=True),
    )(perm_table.T, momenta, energies, orbitals, screened_w)
    return sigma.transpose(0, 2, 1, 3)


def solution(mesh):
    return jax.shard_map(
        shards,
        mesh=mesh,
        in_specs=(P("kgrp", "wrow", None), P(), P(), P(), P(None, None, None, "wrow", None)),
        out_specs=P("kgrp", None, "wrow", None),
        check_vma=False,
    )
```

```python
import functools

import jax
import jax.numpy as jnp
from jax import lax
from jax.experimental import pallas as pl
from jax.experimental.pallas import tpu as pltpu
from jax.sharding import PartitionSpec as P

BETA = 8.0
MESH = pl.DeviceIdType.MESH
NT = (((1,), (1,)), ((), ()))
NN = (((1,), (0,)), ((), ()))


def sign_row(width, first, second):
    half = width // 2
    lane = lax.broadcasted_iota(jnp.int32, (1, width), 1)
    return jnp.where(lane < half, first, second).astype(jnp.float32)


def swap_halves(x):
    half = x.shape[1] // 2
    return jnp.concatenate([x[:, half:], x[:, :half]], axis=1)


def kernel(perm_ref, mom_ref, energy_ref, orb_ref, w_hbm, out_ref,
           xs, kg, wv, scr, lsc, hsend, hrecv, xkt, order, occ,
           rsend, rrecv, fsend, frecv,
           gsend, grecv, ksend, krecv, kcore, hss, hrs, rss, rrs, fss, frs, wsem, osem):
    g = lax.axis_index("kgrp")
    w = lax.axis_index("wrow")
    y, h, c = lax.div(g, 4), lax.rem(lax.div(g, 2), 2), lax.rem(g, 2)
    z, x = lax.div(w, 4), lax.rem(w, 4)
    rows, width = xs.shape[2], xs.shape[3]
    taus = wv.shape[2]

    def wrap(v):
        return lax.rem(v, 4)

    def kdev(y_, h_, c_):
        return y_ * 4 + h_ * 2 + c_

    def wdev(z_, x_):
        return z_ * 4 + x_

    own_x = pltpu.make_async_copy(orb_ref.at[0], xs.at[0, w], osem.at[0])
    own_k = pltpu.make_async_copy(orb_ref.at[0], kg.at[g], osem.at[1])
    own_x.start()
    own_k.start()

    barrier = pltpu.get_barrier_semaphore()
    partner = kdev(y, h, 1 - c)
    across = kdev(y, 1 - h, c)
    up, down = kdev(wrap(y + 1), h, c), kdev(wrap(y + 3), h, c)
    beyond = kdev(wrap(y + 2), h, c)
    for peer in (across, up, down, beyond, partner):
        pl.semaphore_signal(barrier, inc=1, device_id=(peer, w), device_id_type=MESH)
    for d in (2, 1, 3):
        pl.semaphore_signal(barrier, inc=1, device_id=(g, wdev(wrap(z + d), x)), device_id_type=MESH)
        pl.semaphore_signal(barrier, inc=1, device_id=(g, wdev(z, wrap(x + d))), device_id_type=MESH)
    own_x.wait()
    own_k.wait()
    pl.semaphore_wait(barrier, 11)

    def kcopy(block, peer):
        return pltpu.make_async_remote_copy(
            src_ref=kg.at[block], dst_ref=kg.at[block], send_sem=ksend.at[0],
            recv_sem=krecv.at[block], device_id=(peer, w), device_id_type=MESH)

    def kpass(block):
        pltpu.make_async_remote_copy(
            src_ref=kg.at[block], dst_ref=kg.at[block], send_sem=ksend.at[0],
            recv_sem=kcore.at[0], device_id=(partner, w), device_id_type=MESH).start()

    def kwait(block):
        kcopy(block, across).wait_recv()

    def gcopy(s, block, peer):
        return pltpu.make_async_remote_copy(
            src_ref=xs.at[s, block], dst_ref=xs.at[s, block], send_sem=gsend.at[s],
            recv_sem=grecv.at[s, block], device_id=(g, peer), device_id_type=MESH)

    left, right = wdev(z, wrap(x + 3)), wdev(z, wrap(x + 1))

    def gwait(s, block):
        gcopy(s, block, right).wait_recv()

    def gstart_z(s):
        gcopy(s, w, wdev(wrap(z + 1), x)).start()
        gcopy(s, w, wdev(wrap(z + 3), x)).start()
        gcopy(s, w, wdev(wrap(z + 2), x)).start()

    def gstart_x(s):
        gcopy(s, w, right).start()
        gcopy(s, w, left).start()

    def gforward(s, d):
        block = wdev(wrap(z + d), x)
        gwait(s, block)
        gcopy(s, block, right).start()
        gcopy(s, block, left).start()

    def grelay(s, d):
        if d < 2:
            block, peer = wdev(wrap(z + d), wrap(x + 3)), right
        else:
            block, peer = wdev(wrap(z + d), wrap(x + 1)), left
        gwait(s, block)
        gcopy(s, block, peer).start()

    def gfinish(s, d):
        gwait(s, wdev(wrap(z + d), wrap(x + (1 if d < 2 else 3))))
        gwait(s, wdev(wrap(z + d), wrap(x + 2)))

    def kspread(block):
        for peer in (beyond, up, down):
            kcopy(block, peer).start()

    def ktake(yy, hh):
        block = kdev(wrap(y + yy), hh, c)
        kwait(block)
        kpass(block)

    kcopy(g, across).start()
    kspread(g)
    gstart_x(0)
    kpass(g)
    for i in range(4):
        pltpu.make_async_copy(w_hbm.at[i // 2, i % 2], wv.at[i // 2, i % 2], wsem.at[i]).start()
    ktake(1, h)
    gstart_z(0)
    ktake(3, h)
    ktake(2, h)
    grelay(0, 0)
    row = lax.broadcasted_iota(jnp.int32, (192, 192), 0)
    col = lax.broadcasted_iota(jnp.int32, (192, 192), 1)
    part, inner = lax.div(row, 48), lax.rem(row, 48)
    split = lax.div(inner, 12) * 48 + part * 12 + lax.rem(inner, 12)
    tau_row = lax.rem(row, 16)
    merge = lax.rem(tau_row, 4) * 48 + lax.div(tau_row, 4) * 12 + lax.div(row, 16)
    order[0] = jnp.where(col == split, 1.0, 0.0).astype(jnp.bfloat16)
    order[1] = jnp.where(col == merge, 1.0, 0.0).astype(jnp.bfloat16)
    own_row = perm_ref[pl.ds(g, 1), :]
    lane = lax.broadcasted_iota(jnp.int32, own_row.shape, 1)
    sources = [jnp.sum(jnp.where(lane == mom_ref[q], own_row, 0)) for q in range(2)]
    mine = kdev(y, 1 - h, c)
    kwait(mine)
    kspread(mine)
    kpass(mine)
    gforward(0, 1)
    gforward(0, 3)
    gforward(0, 2)
    gfinish(0, 0)
    row = lax.broadcasted_iota(jnp.int32, (width, width), 0)
    col = lax.broadcasted_iota(jnp.int32, (width, width), 1)
    pick = jnp.where(row == col, 1.0, 0.0).astype(jnp.bfloat16)
    strip = xs[0, pl.ds(z * 4, 4)].reshape(4 * rows, width)
    xkt[...] = lax.dot_general(pick, strip, NT, preferred_element_type=jnp.float32).astype(jnp.bfloat16)
    ktake(1, 1 - h)
    ktake(3, 1 - h)
    ktake(2, 1 - h)
    grelay(0, 1)
    grelay(0, 3)
    pltpu.make_async_remote_copy(
        src_ref=kg.at[pl.ds(0, 8)], dst_ref=kg.at[pl.ds(0, 8)], send_sem=ksend.at[0],
        recv_sem=kcore.at[0], device_id=(partner, w), device_id_type=MESH).wait_recv()

    for q in range(2):
        xs[1 + q, w] = kg[sources[q]]
    gstart_z(1)
    gstart_x(1)
    gstart_x(2)

    minus_plus = sign_row(width, -1.0, 1.0)
    plus_minus = sign_row(width, 1.0, -1.0)
    tau = (lax.broadcasted_iota(jnp.int32, (taus, 1), 0).astype(jnp.float32) + 0.5) * (BETA / taus)
    for q in range(2):
        energy = energy_ref[pl.ds(sources[q], 1), :]
        soft = -BETA * energy
        soft = jnp.maximum(soft, 0.0) + jnp.log(1.0 + jnp.exp(-jnp.abs(soft)))
        factor = -jnp.exp(-tau * energy - soft)
        occ[q] = jnp.concatenate([factor, factor], axis=1)

    def tau_of(r, e):
        return r * 4 + wrap(x + e)

    def left_rows(q, r):
        base = xs[1 + q, w].astype(jnp.float32)
        scaled = jnp.concatenate(
            [base * occ[q, pl.ds(tau_of(r, e), 1), :] for e in range(4)], axis=0)
        lsc[q, r, :256] = scaled.astype(jnp.bfloat16)
        lsc[q, r, 256:] = (swap_halves(scaled) * plus_minus).astype(jnp.bfloat16)

    def left_round(r, carry):
        left_rows(0, r)
        left_rows(1, r)
        return carry

    lax.fori_loop(0, 4, left_round, 0, unroll=True)
    grelay(0, 2)

    def screen(q, n, r):
        cols = pl.ds(pl.multiple_of(n * 256, 256), 256)
        tile = xs[1 + q, pl.ds(n * 4, 4)].reshape(256, width)
        green = lax.dot_general(lsc[q, r], tile, NT, preferred_element_type=jnp.float32)
        for e in range(4):
            t = tau_of(r, e)
            real_rows, imag_rows = slice(e * 64, e * 64 + 64), slice(256 + e * 64, 320 + e * 64)
            gr, gi = green[real_rows], green[imag_rows]
            wr = wv[q, 0, t, :, cols].astype(jnp.float32)
            wi = wv[q, 1, t, :, cols].astype(jnp.float32)
            sr = gr * wr - gi * wi
            si = gr * wi + gi * wr
            if q == 1:
                sr = sr + scr[r, real_rows, cols].astype(jnp.float32)
                si = si + scr[r, imag_rows, cols].astype(jnp.float32)
            scr[r, real_rows, cols] = sr.astype(jnp.bfloat16)
            scr[r, imag_rows, cols] = si.astype(jnp.bfloat16)

    def tile(q, d):
        n = wrap(z + d)

        def one_round(r, carry):
            screen(q, n, r)
            return carry

        lax.fori_loop(0, 4, one_round, 0, unroll=True)

    gstart_z(2)
    grelay(1, 0)
    gforward(1, 1)
    gforward(1, 3)
    grelay(2, 0)
    gforward(1, 2)
    for i in range(2):
        pltpu.make_async_copy(w_hbm.at[0, i], wv.at[0, i], wsem.at[i]).wait()
    grelay(1, 1)
    grelay(1, 3)
    gfinish(1, 0)
    tile(0, 0)
    gforward(2, 1)
    gforward(2, 3)
    grelay(1, 2)
    gfinish(1, 1)
    tile(0, 1)
    gforward(2, 2)
    gfinish(1, 3)
    tile(0, 3)
    grelay(2, 1)
    grelay(2, 3)
    gfinish(1, 2)
    tile(0, 2)
    for i in range(2):
        pltpu.make_async_copy(w_hbm.at[1, i], wv.at[1, i], wsem.at[2 + i]).wait()
    gfinish(2, 0)
    tile(1, 0)
    grelay(2, 2)
    gfinish(2, 1)
    tile(1, 1)
    gfinish(2, 3)
    tile(1, 3)
    gfinish(2, 2)
    for d in (1, 3, 2):
        gfinish(0, d)

    def hcopy(r, e):
        return pltpu.make_async_remote_copy(
            src_ref=hsend.at[r, e], dst_ref=hrecv.at[r, x], send_sem=hss.at[0],
            recv_sem=hrs.at[r], device_id=(g, wdev(z, wrap(x + e))), device_id_type=MESH)

    def last(r, carry):
        screen(1, wrap(z + 2), r)
        both = lax.dot_general(scr[r], xs[0].reshape(16 * rows, width), NN,
                               preferred_element_type=jnp.float32)
        half = both[:256] + swap_halves(both[256:]) * minus_plus
        half = half.astype(jnp.bfloat16)
        for e in (2, 1, 3):
            hsend[r, e] = half[e * 64:e * 64 + 64]
        hrecv[r, x] = half[:64]
        for e in (2, 1, 3):
            hcopy(r, e).start()
        return carry

    lax.fori_loop(0, 4, last, 0, unroll=True)

    def rcopy(r, d):
        other = wrap(z + d)
        return pltpu.make_async_remote_copy(
            src_ref=rsend.at[r, other], dst_ref=rrecv.at[r, z], send_sem=rss.at[0],
            recv_sem=rrs.at[0], device_id=(g, wdev(other, x)), device_id_type=MESH)

    def project(r):
        pltpu.make_async_remote_copy(
            src_ref=hrecv.at[r, pl.ds(0, 3)], dst_ref=hrecv.at[r, pl.ds(0, 3)], send_sem=hss.at[0],
            recv_sem=hrs.at[r], device_id=(g, right), device_id_type=MESH).wait_recv()
        total = lax.dot_general(xkt[...], hrecv[r].reshape(4 * rows, width), NN,
                                preferred_element_type=jnp.float32)
        sigma = total[:192] + swap_halves(total[192:]) * plus_minus
        sigma = sigma.reshape(4, 48, width)
        rsend[r] = sigma.astype(jnp.bfloat16)
        for d in (2, 1, 3):
            rcopy(r, d).start()

    for r in range(4):
        project(r)

    pltpu.make_async_remote_copy(
        src_ref=rrecv.at[pl.ds(0, 3)], dst_ref=rrecv.at[pl.ds(0, 3)], send_sem=rss.at[0],
        recv_sem=rrs.at[0], device_id=(g, right), device_id_type=MESH).wait_recv()
    sums = []
    for r in range(4):
        total = rsend[r, z].astype(jnp.float32)
        for d in range(1, 4):
            total = total + rrecv[r, wrap(z + d)].astype(jnp.float32)
        sums.append(total)
    summed = jnp.concatenate(sums, axis=0).astype(jnp.bfloat16)
    pieces = lax.dot_general(order[0], summed, NN, preferred_element_type=jnp.float32)
    fsend[...] = pieces.astype(jnp.bfloat16).reshape(4, 48, width)
    frecv[x] = fsend[x]
    for e in (2, 1, 3):
        other = wrap(x + e)
        pltpu.make_async_remote_copy(
            src_ref=fsend.at[other], dst_ref=frecv.at[x], send_sem=fss.at[0],
            recv_sem=frs.at[0], device_id=(g, wdev(z, other)), device_id_type=MESH).start()

    for s in range(3):
        pltpu.make_async_remote_copy(
            src_ref=xs.at[s, pl.ds(0, 15)], dst_ref=xs.at[s, pl.ds(0, 15)], send_sem=gsend.at[s],
            recv_sem=grecv.at[s, 0], device_id=(g, right), device_id_type=MESH).wait_send()
    pltpu.make_async_remote_copy(
        src_ref=kg.at[pl.ds(0, 15)], dst_ref=kg.at[pl.ds(0, 15)], send_sem=ksend.at[0],
        recv_sem=kcore.at[0], device_id=(partner, w), device_id_type=MESH).wait_send()
    pltpu.make_async_remote_copy(
        src_ref=hsend.at[pl.ds(0, 3)], dst_ref=hrecv.at[pl.ds(0, 3)], send_sem=hss.at[0],
        recv_sem=hrs.at[0], device_id=(g, right), device_id_type=MESH).wait_send()
    pltpu.make_async_remote_copy(
        src_ref=rsend.at[pl.ds(0, 3)], dst_ref=rrecv.at[pl.ds(0, 3)], send_sem=rss.at[0],
        recv_sem=rrs.at[0], device_id=(g, right), device_id_type=MESH).wait_send()
    pltpu.make_async_remote_copy(
        src_ref=fsend.at[pl.ds(0, 3)], dst_ref=frecv.at[pl.ds(0, 3)], send_sem=fss.at[0],
        recv_sem=frs.at[0], device_id=(g, right), device_id_type=MESH).wait()
    out_ref[0] = lax.dot_general(order[1], frecv[...].reshape(192, width), NN,
                                 preferred_element_type=jnp.float32).reshape(12, 16, width)


def shards(orbitals, energies, perm_table, momenta, screened_w):
    _, rows, width = orbitals.shape
    taus, points = screened_w.shape[2], screened_w.shape[4]
    bf16, f32 = jnp.bfloat16, jnp.float32
    dma = pltpu.SemaphoreType.DMA
    smem = pl.BlockSpec(memory_space=pltpu.SMEM)
    vmem = pl.BlockSpec(memory_space=pltpu.VMEM)
    sigma = pl.pallas_call(
        kernel,
        out_shape=jax.ShapeDtypeStruct((1, 12, taus, width), f32),
        in_specs=[vmem, smem, vmem, pl.BlockSpec(memory_space=pl.ANY), pl.BlockSpec(memory_space=pl.ANY)],
        out_specs=vmem,
        scratch_shapes=[
            pltpu.VMEM((3, 16, rows, width), bf16),
            pltpu.VMEM((16, rows, width), bf16),
            pltpu.VMEM((2, 2, taus, rows, points), bf16),
            pltpu.VMEM((4, 512, points), bf16),
            pltpu.VMEM((2, 4, 512, width), bf16),
            pltpu.VMEM((4, 4, rows, width), bf16),
            pltpu.VMEM((4, 4, rows, width), bf16),
            pltpu.VMEM((width, 4 * rows), bf16),
            pltpu.VMEM((2, 192, 192), bf16),
            pltpu.VMEM((2, taus, width), f32),
            pltpu.VMEM((4, 4, 48, width), bf16),
            pltpu.VMEM((4, 4, 48, width), bf16),
            pltpu.VMEM((4, 48, width), bf16),
            pltpu.VMEM((4, 48, width), bf16),
            dma((3,)), dma((3, 16)), dma((1,)), dma((16,)), dma((1,)),
            dma((1,)), dma((4,)), dma((1,)), dma((1,)), dma((1,)), dma((1,)),
            dma((4,)), dma((2,)),
        ],
        compiler_params=pltpu.CompilerParams(collective_id=0, has_side_effects=True),
    )(perm_table.T, momenta, energies, orbitals, screened_w)
    return sigma.transpose(0, 2, 1, 3)


def solution(mesh):
    return jax.shard_map(
        shards,
        mesh=mesh,
        in_specs=(P("kgrp", "wrow", None), P(), P(), P(), P(None, None, None, "wrow", None)),
        out_specs=P("kgrp", None, "wrow", None),
        check_vma=False,
    )
```

```python
import functools

import jax
import jax.numpy as jnp
from jax import lax
from jax.experimental import pallas as pl
from jax.experimental.pallas import tpu as pltpu
from jax.sharding import PartitionSpec as P

BETA = 8.0
MESH = pl.DeviceIdType.MESH
NT = (((1,), (1,)), ((), ()))
NN = (((1,), (0,)), ((), ()))


def sign_row(width, first, second):
    half = width // 2
    lane = lax.broadcasted_iota(jnp.int32, (1, width), 1)
    return jnp.where(lane < half, first, second).astype(jnp.float32)


def pack_columns(x):
    return jnp.concatenate([x[:, :192], x[:, 320:], x[:, 192:320]], axis=1)


def unpack_columns(x):
    return jnp.concatenate([x[:, :192], x[:, 256:], x[:, 192:256]], axis=1)


def swap_halves(x):
    return jnp.concatenate([x[:, 256:], pltpu.roll(x[:, 128:256], 64, axis=1), x[:, :128]], axis=1)


def kernel(perm_hbm, mom_hbm, energy_hbm, orb_ref, w_hbm, out_ref,
           perm_ref, mom_ref, energy_ref, own, xs, kg, wv, scr, lsc, hsend, hrecv, xkt, order, occ,
           rsend, rrecv, fsend, frecv,
           gsend, grecv, ksend, krecv, kcore, hss, hrs, rss, rrs, fss, frs, wsem, osem):
    g = lax.axis_index("kgrp")
    w = lax.axis_index("wrow")
    y, h, c = lax.div(g, 4), lax.rem(lax.div(g, 2), 2), lax.rem(g, 2)
    z, x = lax.div(w, 4), lax.rem(w, 4)
    rows, width = xs.shape[2], xs.shape[3]
    taus = wv.shape[2]

    def wrap(v):
        return lax.rem(v, 4)

    def kdev(y_, h_, c_):
        return y_ * 4 + h_ * 2 + c_

    def wdev(z_, x_):
        return z_ * 4 + x_

    own_rows = pltpu.make_async_copy(orb_ref.at[0], own, osem.at[0])
    tables = [
        pltpu.make_async_copy(src, dst, osem.at[1 + i])
        for i, (src, dst) in enumerate(((perm_hbm, perm_ref), (mom_hbm, mom_ref), (energy_hbm, energy_ref)))]
    own_rows.start()
    for table in tables:
        table.start()

    barrier = pltpu.get_barrier_semaphore()
    partner = kdev(y, h, 1 - c)
    across = kdev(y, 1 - h, c)
    up, down = kdev(wrap(y + 1), h, c), kdev(wrap(y + 3), h, c)
    beyond = kdev(wrap(y + 2), h, c)
    for peer in (across, up, down, beyond, partner):
        pl.semaphore_signal(barrier, inc=1, device_id=(peer, w), device_id_type=MESH)
    for d in (2, 1, 3):
        pl.semaphore_signal(barrier, inc=1, device_id=(g, wdev(wrap(z + d), x)), device_id_type=MESH)
        pl.semaphore_signal(barrier, inc=1, device_id=(g, wdev(z, wrap(x + d))), device_id_type=MESH)
    own_rows.wait()
    packed = pack_columns(own[...])
    xs[0, w] = packed
    kg[g] = packed
    pl.semaphore_wait(barrier, 11)

    def kcopy(block, peer):
        return pltpu.make_async_remote_copy(
            src_ref=kg.at[block], dst_ref=kg.at[block], send_sem=ksend.at[0],
            recv_sem=krecv.at[block], device_id=(peer, w), device_id_type=MESH)

    def kpass(block):
        pltpu.make_async_remote_copy(
            src_ref=kg.at[block], dst_ref=kg.at[block], send_sem=ksend.at[0],
            recv_sem=kcore.at[0], device_id=(partner, w), device_id_type=MESH).start()

    def kwait(block):
        kcopy(block, across).wait_recv()

    def gcopy(s, block, peer):
        return pltpu.make_async_remote_copy(
            src_ref=xs.at[s, block], dst_ref=xs.at[s, block], send_sem=gsend.at[s],
            recv_sem=grecv.at[s, block], device_id=(g, peer), device_id_type=MESH)

    left, right = wdev(z, wrap(x + 3)), wdev(z, wrap(x + 1))

    def gwait(s, block):
        gcopy(s, block, right).wait_recv()

    def gstart_z(s):
        gcopy(s, w, wdev(wrap(z + 1), x)).start()
        gcopy(s, w, wdev(wrap(z + 3), x)).start()
        gcopy(s, w, wdev(wrap(z + 2), x)).start()

    def gstart_x(s):
        gcopy(s, w, right).start()
        gcopy(s, w, left).start()

    def gforward(s, d):
        block = wdev(wrap(z + d), x)
        gwait(s, block)
        gcopy(s, block, right).start()
        gcopy(s, block, left).start()

    def grelay(s, d):
        if d < 2:
            block, peer = wdev(wrap(z + d), wrap(x + 3)), right
        else:
            block, peer = wdev(wrap(z + d), wrap(x + 1)), left
        gwait(s, block)
        gcopy(s, block, peer).start()

    def gfinish(s, d):
        gwait(s, wdev(wrap(z + d), wrap(x + (1 if d < 2 else 3))))
        gwait(s, wdev(wrap(z + d), wrap(x + 2)))

    def kspread(block):
        for peer in (beyond, up, down):
            kcopy(block, peer).start()

    def ktake(yy, hh):
        block = kdev(wrap(y + yy), hh, c)
        kwait(block)
        kpass(block)

    kcopy(g, across).start()
    kspread(g)
    gstart_x(0)
    kpass(g)
    for i in range(4):
        pltpu.make_async_copy(w_hbm.at[i // 2, i % 2], wv.at[i // 2, i % 2], wsem.at[i]).start()
    ktake(1, h)
    gstart_z(0)
    ktake(3, h)
    ktake(2, h)
    grelay(0, 0)
    row = lax.broadcasted_iota(jnp.int32, (192, 192), 0)
    col = lax.broadcasted_iota(jnp.int32, (192, 192), 1)
    part, inner = lax.div(row, 48), lax.rem(row, 48)
    split = lax.div(inner, 12) * 48 + part * 12 + lax.rem(inner, 12)
    tau_row = lax.rem(row, 16)
    merge = lax.rem(tau_row, 4) * 48 + lax.div(tau_row, 4) * 12 + lax.div(row, 16)
    order[0] = jnp.where(col == split, 1.0, 0.0).astype(jnp.bfloat16)
    order[1] = jnp.where(col == merge, 1.0, 0.0).astype(jnp.bfloat16)
    for table in tables:
        table.wait()
    own_row = perm_ref[pl.ds(g, 1), :]
    lane = lax.broadcasted_iota(jnp.int32, own_row.shape, 1)
    sources = [jnp.sum(jnp.where(lane == mom_ref[q], own_row, 0)) for q in range(2)]
    mine = kdev(y, 1 - h, c)
    kwait(mine)
    kspread(mine)
    kpass(mine)
    gforward(0, 1)
    gforward(0, 3)
    gforward(0, 2)
    gfinish(0, 0)
    row = lax.broadcasted_iota(jnp.int32, (width, width), 0)
    col = lax.broadcasted_iota(jnp.int32, (width, width), 1)
    want = jnp.where(row < 192, row, 192 + lax.rem(row + 64, 192))
    pick = jnp.where(want == col, 1.0, 0.0).astype(jnp.bfloat16)
    strip = xs[0, pl.ds(z * 4, 4)].reshape(4 * rows, width)
    xkt[...] = lax.dot_general(pick, strip, NT, preferred_element_type=jnp.float32).astype(jnp.bfloat16)
    ktake(1, 1 - h)
    ktake(3, 1 - h)
    ktake(2, 1 - h)
    grelay(0, 1)
    grelay(0, 3)
    pltpu.make_async_remote_copy(
        src_ref=kg.at[pl.ds(0, 8)], dst_ref=kg.at[pl.ds(0, 8)], send_sem=ksend.at[0],
        recv_sem=kcore.at[0], device_id=(partner, w), device_id_type=MESH).wait_recv()

    for q in range(2):
        xs[1 + q, w] = kg[sources[q]]
    gstart_z(1)
    gstart_x(1)
    gstart_x(2)

    minus_plus = sign_row(width, -1.0, 1.0)
    plus_minus = sign_row(width, 1.0, -1.0)
    tau = (lax.broadcasted_iota(jnp.int32, (taus, 1), 0).astype(jnp.float32) + 0.5) * (BETA / taus)
    for q in range(2):
        energy = energy_ref[pl.ds(sources[q], 1), :]
        soft = -BETA * energy
        soft = jnp.maximum(soft, 0.0) + jnp.log(1.0 + jnp.exp(-jnp.abs(soft)))
        factor = -jnp.exp(-tau * energy - soft)
        occ[q] = pack_columns(jnp.concatenate([factor, factor], axis=1))

    def tau_of(r, e):
        return r * 4 + wrap(x + e)

    def left_rows(q, r):
        base = xs[1 + q, w].astype(jnp.float32)
        scaled = jnp.concatenate(
            [base * occ[q, pl.ds(tau_of(r, e), 1), :] for e in range(4)], axis=0)
        lsc[q, r, :256] = scaled.astype(jnp.bfloat16)
        lsc[q, r, 256:] = (swap_halves(scaled) * plus_minus).astype(jnp.bfloat16)

    def left_round(r, carry):
        left_rows(0, r)
        left_rows(1, r)
        return carry

    lax.fori_loop(0, 4, left_round, 0, unroll=True)
    grelay(0, 2)

    def screen(q, n, r):
        cols = pl.ds(pl.multiple_of(n * 256, 256), 256)
        tile = xs[1 + q, pl.ds(n * 4, 4)].reshape(256, width)
        green = lax.dot_general(lsc[q, r], tile, NT, preferred_element_type=jnp.float32)
        for e in range(4):
            t = tau_of(r, e)
            real_rows, imag_rows = slice(e * 64, e * 64 + 64), slice(256 + e * 64, 320 + e * 64)
            gr, gi = green[real_rows], green[imag_rows]
            wr = wv[q, 0, t, :, cols].astype(jnp.float32)
            wi = wv[q, 1, t, :, cols].astype(jnp.float32)
            sr = gr * wr - gi * wi
            si = gr * wi + gi * wr
            if q == 1:
                sr = sr + scr[r, real_rows, cols].astype(jnp.float32)
                si = si + scr[r, imag_rows, cols].astype(jnp.float32)
            scr[r, real_rows, cols] = sr.astype(jnp.bfloat16)
            scr[r, imag_rows, cols] = si.astype(jnp.bfloat16)

    def tile(q, d):
        n = wrap(z + d)

        def one_round(r, carry):
            screen(q, n, r)
            return carry

        lax.fori_loop(0, 4, one_round, 0, unroll=True)

    gstart_z(2)
    grelay(1, 0)
    gforward(1, 1)
    gforward(1, 3)
    grelay(2, 0)
    gforward(1, 2)
    for i in range(2):
        pltpu.make_async_copy(w_hbm.at[0, i], wv.at[0, i], wsem.at[i]).wait()
    gfinish(1, 0)
    tile(0, 0)
    grelay(1, 1)
    grelay(1, 3)
    gforward(2, 1)
    gforward(2, 3)
    gforward(2, 2)
    grelay(1, 2)
    gfinish(1, 1)
    tile(0, 1)
    gfinish(1, 3)
    tile(0, 3)
    grelay(2, 1)
    grelay(2, 3)
    gfinish(1, 2)
    tile(0, 2)
    grelay(2, 2)
    for i in range(2):
        pltpu.make_async_copy(w_hbm.at[1, i], wv.at[1, i], wsem.at[2 + i]).wait()
    gfinish(2, 0)
    tile(1, 0)
    gfinish(2, 1)
    tile(1, 1)
    gfinish(2, 3)
    tile(1, 3)
    gfinish(2, 2)
    for d in (1, 3, 2):
        gfinish(0, d)

    def hcopy(r, e):
        return pltpu.make_async_remote_copy(
            src_ref=hsend.at[r, e], dst_ref=hrecv.at[r, x], send_sem=hss.at[0],
            recv_sem=hrs.at[r], device_id=(g, wdev(z, wrap(x + e))), device_id_type=MESH)

    def last(r, carry):
        screen(1, wrap(z + 2), r)
        both = lax.dot_general(scr[r], xs[0].reshape(16 * rows, width), NN,
                               preferred_element_type=jnp.float32)
        half = both[:256] + swap_halves(both[256:]) * minus_plus
        half = half.astype(jnp.bfloat16)
        for e in (2, 1, 3):
            hsend[r, e] = half[e * 64:e * 64 + 64]
        hrecv[r, x] = half[:64]
        for e in (2, 1, 3):
            hcopy(r, e).start()
        return carry

    lax.fori_loop(0, 4, last, 0, unroll=True)

    def rcopy(r, d):
        other = wrap(z + d)
        return pltpu.make_async_remote_copy(
            src_ref=rsend.at[r, other], dst_ref=rrecv.at[r, z], send_sem=rss.at[0],
            recv_sem=rrs.at[0], device_id=(g, wdev(other, x)), device_id_type=MESH)

    def project(r):
        pltpu.make_async_remote_copy(
            src_ref=hrecv.at[r, pl.ds(0, 3)], dst_ref=hrecv.at[r, pl.ds(0, 3)], send_sem=hss.at[0],
            recv_sem=hrs.at[r], device_id=(g, right), device_id_type=MESH).wait_recv()
        total = lax.dot_general(xkt[...], hrecv[r].reshape(4 * rows, width), NN,
                                preferred_element_type=jnp.float32)
        sigma = total[:192] + swap_halves(total[192:]) * plus_minus
        sigma = sigma.reshape(4, 48, width)
        rsend[r] = sigma.astype(jnp.bfloat16)
        for d in (2, 1, 3):
            rcopy(r, d).start()

    for r in range(4):
        project(r)

    pltpu.make_async_remote_copy(
        src_ref=rrecv.at[pl.ds(0, 3)], dst_ref=rrecv.at[pl.ds(0, 3)], send_sem=rss.at[0],
        recv_sem=rrs.at[0], device_id=(g, right), device_id_type=MESH).wait_recv()
    sums = []
    for r in range(4):
        total = rsend[r, z].astype(jnp.float32)
        for d in range(1, 4):
            total = total + rrecv[r, wrap(z + d)].astype(jnp.float32)
        sums.append(total)
    summed = jnp.concatenate(sums, axis=0).astype(jnp.bfloat16)
    pieces = lax.dot_general(order[0], summed, NN, preferred_element_type=jnp.float32)
    fsend[...] = pieces.astype(jnp.bfloat16).reshape(4, 48, width)
    frecv[x] = fsend[x]
    for e in (2, 1, 3):
        other = wrap(x + e)
        pltpu.make_async_remote_copy(
            src_ref=fsend.at[other], dst_ref=frecv.at[x], send_sem=fss.at[0],
            recv_sem=frs.at[0], device_id=(g, wdev(z, other)), device_id_type=MESH).start()

    for s in range(3):
        pltpu.make_async_remote_copy(
            src_ref=xs.at[s, pl.ds(0, 15)], dst_ref=xs.at[s, pl.ds(0, 15)], send_sem=gsend.at[s],
            recv_sem=grecv.at[s, 0], device_id=(g, right), device_id_type=MESH).wait_send()
    pltpu.make_async_remote_copy(
        src_ref=kg.at[pl.ds(0, 15)], dst_ref=kg.at[pl.ds(0, 15)], send_sem=ksend.at[0],
        recv_sem=kcore.at[0], device_id=(partner, w), device_id_type=MESH).wait_send()
    pltpu.make_async_remote_copy(
        src_ref=hsend.at[pl.ds(0, 3)], dst_ref=hrecv.at[pl.ds(0, 3)], send_sem=hss.at[0],
        recv_sem=hrs.at[0], device_id=(g, right), device_id_type=MESH).wait_send()
    pltpu.make_async_remote_copy(
        src_ref=rsend.at[pl.ds(0, 3)], dst_ref=rrecv.at[pl.ds(0, 3)], send_sem=rss.at[0],
        recv_sem=rrs.at[0], device_id=(g, right), device_id_type=MESH).wait_send()
    pltpu.make_async_remote_copy(
        src_ref=fsend.at[pl.ds(0, 3)], dst_ref=frecv.at[pl.ds(0, 3)], send_sem=fss.at[0],
        recv_sem=frs.at[0], device_id=(g, right), device_id_type=MESH).wait()
    result = lax.dot_general(order[1], frecv[...].reshape(192, width), NN,
                             preferred_element_type=jnp.float32)
    out_ref[0] = unpack_columns(result).reshape(12, 16, width)


def shards(orbitals, energies, perm_table, momenta, screened_w):
    _, rows, width = orbitals.shape
    taus, points = screened_w.shape[2], screened_w.shape[4]
    bf16, f32 = jnp.bfloat16, jnp.float32
    dma = pltpu.SemaphoreType.DMA
    hbm = pl.BlockSpec(memory_space=pltpu.HBM)
    vmem = pl.BlockSpec(memory_space=pltpu.VMEM)
    sigma = pl.pallas_call(
        kernel,
        out_shape=jax.ShapeDtypeStruct((1, 12, taus, width), f32),
        in_specs=[hbm] * 5,
        out_specs=vmem,
        scratch_shapes=[
            pltpu.VMEM(perm_table.shape[::-1], jnp.int32),
            pltpu.SMEM(momenta.shape, jnp.int32),
            pltpu.VMEM(energies.shape, f32),
            pltpu.VMEM((rows, width), bf16),
            pltpu.VMEM((3, 16, rows, width), bf16),
            pltpu.VMEM((16, rows, width), bf16),
            pltpu.VMEM((2, 2, taus, rows, points), bf16),
            pltpu.VMEM((4, 512, points), bf16),
            pltpu.VMEM((2, 4, 512, width), bf16),
            pltpu.VMEM((4, 4, rows, width), bf16),
            pltpu.VMEM((4, 4, rows, width), bf16),
            pltpu.VMEM((width, 4 * rows), bf16),
            pltpu.VMEM((2, 192, 192), bf16),
            pltpu.VMEM((2, taus, width), f32),
            pltpu.VMEM((4, 4, 48, width), bf16),
            pltpu.VMEM((4, 4, 48, width), bf16),
            pltpu.VMEM((4, 48, width), bf16),
            pltpu.VMEM((4, 48, width), bf16),
            dma((3,)), dma((3, 16)), dma((1,)), dma((16,)), dma((1,)),
            dma((1,)), dma((4,)), dma((1,)), dma((1,)), dma((1,)), dma((1,)),
            dma((4,)), dma((4,)),
        ],
        compiler_params=pltpu.CompilerParams(collective_id=0, has_side_effects=True, vmem_limit_bytes=40 * 2**20),
    )(*[pltpu.with_memory_space_constraint(a, pltpu.HBM)
        for a in (perm_table.T, momenta, energies, orbitals, screened_w)])
    return sigma.transpose(0, 2, 1, 3)


def solution(mesh):
    return jax.shard_map(
        shards,
        mesh=mesh,
        in_specs=(P("kgrp", "wrow", None), P(), P(), P(), P(None, None, None, "wrow", None)),
        out_specs=P("kgrp", None, "wrow", None),
        check_vma=False,
    )
```

```python
import functools

import jax
import jax.numpy as jnp
from jax import lax
from jax.experimental import pallas as pl
from jax.experimental.pallas import tpu as pltpu
from jax.sharding import PartitionSpec as P

BETA = 8.0
MESH = pl.DeviceIdType.MESH
NT = (((1,), (1,)), ((), ()))
NN = (((1,), (0,)), ((), ()))


def sign_row(width, first, second):
    half = width // 2
    lane = lax.broadcasted_iota(jnp.int32, (1, width), 1)
    return jnp.where(lane < half, first, second).astype(jnp.float32)


def pack_columns(x):
    return jnp.concatenate([x[:, :192], x[:, 320:], x[:, 192:320]], axis=1)


def unpack_columns(x):
    return jnp.concatenate([x[:, :192], x[:, 256:], x[:, 192:256]], axis=1)


def swap_halves(x):
    return jnp.concatenate([x[:, 256:], pltpu.roll(x[:, 128:256], 64, axis=1), x[:, :128]], axis=1)


def kernel(perm_hbm, mom_hbm, energy_hbm, orb_ref, w_hbm, out_ref,
           perm_ref, mom_ref, energy_ref, own, xs, kg, wv, scr, lsc, hsend, hrecv, xkt, order, unorder, occ,
           rsend, rrecv, fsend, frecv, fwait,
           gsend, grecv, ksend, krecv, kcore, hss, hrs, rss, rrs, fss, frs, wsem, osem):
    g = lax.axis_index("kgrp")
    w = lax.axis_index("wrow")
    y, h, c = lax.div(g, 4), lax.rem(lax.div(g, 2), 2), lax.rem(g, 2)
    z, x = lax.div(w, 4), lax.rem(w, 4)
    rows, width = xs.shape[2], xs.shape[3]
    taus = wv.shape[2]

    def wrap(v):
        return lax.rem(v, 4)

    def kdev(y_, h_, c_):
        return y_ * 4 + h_ * 2 + c_

    def wdev(z_, x_):
        return z_ * 4 + x_

    own_rows = pltpu.make_async_copy(orb_ref.at[0], own, osem.at[0])
    tables = [
        pltpu.make_async_copy(src, dst, osem.at[1 + i])
        for i, (src, dst) in enumerate(((perm_hbm, perm_ref), (mom_hbm, mom_ref), (energy_hbm, energy_ref)))]
    own_rows.start()
    for table in tables:
        table.start()

    barrier = pltpu.get_barrier_semaphore()
    partner = kdev(y, h, 1 - c)
    across = kdev(y, 1 - h, c)
    up, down = kdev(wrap(y + 1), h, c), kdev(wrap(y + 3), h, c)
    beyond = kdev(wrap(y + 2), h, c)
    for peer in (across, up, down, beyond, partner):
        pl.semaphore_signal(barrier, inc=1, device_id=(peer, w), device_id_type=MESH)
    for d in (2, 1, 3):
        pl.semaphore_signal(barrier, inc=1, device_id=(g, wdev(wrap(z + d), x)), device_id_type=MESH)
        pl.semaphore_signal(barrier, inc=1, device_id=(g, wdev(z, wrap(x + d))), device_id_type=MESH)
    own_rows.wait()
    packed = pack_columns(own[...])
    xs[0, w] = packed
    kg[g] = packed
    pl.semaphore_wait(barrier, 11)

    def kcopy(block, peer):
        return pltpu.make_async_remote_copy(
            src_ref=kg.at[block], dst_ref=kg.at[block], send_sem=ksend.at[0],
            recv_sem=krecv.at[block], device_id=(peer, w), device_id_type=MESH)

    def kpass(block):
        pltpu.make_async_remote_copy(
            src_ref=kg.at[block], dst_ref=kg.at[block], send_sem=ksend.at[0],
            recv_sem=kcore.at[0], device_id=(partner, w), device_id_type=MESH).start()

    def kwait(block):
        kcopy(block, across).wait_recv()

    def gcopy(s, block, peer):
        return pltpu.make_async_remote_copy(
            src_ref=xs.at[s, block], dst_ref=xs.at[s, block], send_sem=gsend.at[s],
            recv_sem=grecv.at[s, block], device_id=(g, peer), device_id_type=MESH)

    left, right = wdev(z, wrap(x + 3)), wdev(z, wrap(x + 1))

    def gwait(s, block):
        gcopy(s, block, right).wait_recv()

    def gstart_z(s):
        gcopy(s, w, wdev(wrap(z + 1), x)).start()
        gcopy(s, w, wdev(wrap(z + 3), x)).start()
        gcopy(s, w, wdev(wrap(z + 2), x)).start()

    def gstart_x(s):
        gcopy(s, w, right).start()
        gcopy(s, w, left).start()

    def gforward(s, d):
        block = wdev(wrap(z + d), x)
        gwait(s, block)
        gcopy(s, block, right).start()
        gcopy(s, block, left).start()

    def grelay(s, d):
        if d < 2:
            block, peer = wdev(wrap(z + d), wrap(x + 3)), right
        else:
            block, peer = wdev(wrap(z + d), wrap(x + 1)), left
        gwait(s, block)
        gcopy(s, block, peer).start()

    def gfinish(s, d):
        gwait(s, wdev(wrap(z + d), wrap(x + (1 if d < 2 else 3))))
        gwait(s, wdev(wrap(z + d), wrap(x + 2)))

    def kspread(block):
        for peer in (beyond, up, down):
            kcopy(block, peer).start()

    def ktake(yy, hh):
        block = kdev(wrap(y + yy), hh, c)
        kwait(block)
        kpass(block)

    kcopy(g, across).start()
    kspread(g)
    gstart_x(0)
    kpass(g)
    for i in range(4):
        pltpu.make_async_copy(w_hbm.at[i // 2, i % 2], wv.at[i // 2, i % 2], wsem.at[i]).start()
    ktake(1, h)
    gstart_z(0)
    ktake(3, h)
    ktake(2, h)
    grelay(0, 0)
    row = lax.broadcasted_iota(jnp.int32, (96, 96), 0)
    col = lax.broadcasted_iota(jnp.int32, (96, 96), 1)
    part, inner = lax.div(row, 24), lax.rem(row, 24)
    split = lax.div(inner, 12) * 48 + part * 12 + lax.rem(inner, 12)
    order[...] = jnp.where(col == split, 1.0, 0.0).astype(jnp.bfloat16)
    row = lax.broadcasted_iota(jnp.int32, (192, 192), 0)
    col = lax.broadcasted_iota(jnp.int32, (192, 192), 1)
    tau_row = lax.rem(row, 16)
    late, odd = lax.div(tau_row, 8), lax.rem(lax.div(tau_row, 4), 2)
    merge = late * 96 + lax.rem(tau_row, 4) * 24 + odd * 12 + lax.div(row, 16)
    unorder[...] = jnp.where(col == merge, 1.0, 0.0).astype(jnp.bfloat16)
    for table in tables:
        table.wait()
    own_row = perm_ref[pl.ds(g, 1), :]
    lane = lax.broadcasted_iota(jnp.int32, own_row.shape, 1)
    sources = [jnp.sum(jnp.where(lane == mom_ref[q], own_row, 0)) for q in range(2)]
    mine = kdev(y, 1 - h, c)
    kwait(mine)
    kspread(mine)
    kpass(mine)
    gforward(0, 1)
    gforward(0, 3)
    ktake(1, 1 - h)
    ktake(3, 1 - h)
    ktake(2, 1 - h)
    gforward(0, 2)
    gfinish(0, 0)
    row = lax.broadcasted_iota(jnp.int32, (width, width), 0)
    col = lax.broadcasted_iota(jnp.int32, (width, width), 1)
    want = jnp.where(row < 192, row, 192 + lax.rem(row + 64, 192))
    pick = jnp.where(want == col, 1.0, 0.0).astype(jnp.bfloat16)
    strip = xs[0, pl.ds(z * 4, 4)].reshape(4 * rows, width)
    xkt[...] = lax.dot_general(pick, strip, NT, preferred_element_type=jnp.float32).astype(jnp.bfloat16)
    grelay(0, 1)
    pltpu.make_async_remote_copy(
        src_ref=kg.at[pl.ds(0, 8)], dst_ref=kg.at[pl.ds(0, 8)], send_sem=ksend.at[0],
        recv_sem=kcore.at[0], device_id=(partner, w), device_id_type=MESH).wait_recv()

    for q in range(2):
        xs[1 + q, w] = kg[sources[q]]
    gstart_z(1)
    gstart_x(1)
    gstart_x(2)

    minus_plus = sign_row(width, -1.0, 1.0)
    plus_minus = sign_row(width, 1.0, -1.0)
    tau = (lax.broadcasted_iota(jnp.int32, (taus, 1), 0).astype(jnp.float32) + 0.5) * (BETA / taus)
    for q in range(2):
        energy = energy_ref[pl.ds(sources[q], 1), :]
        soft = -BETA * energy
        soft = jnp.maximum(soft, 0.0) + jnp.log(1.0 + jnp.exp(-jnp.abs(soft)))
        factor = -jnp.exp(-tau * energy - soft)
        occ[q] = pack_columns(jnp.concatenate([factor, factor], axis=1))

    def tau_of(r, e):
        return r * 4 + wrap(x + e)

    def left_rows(q, r):
        base = xs[1 + q, w].astype(jnp.float32)
        scaled = jnp.concatenate(
            [base * occ[q, pl.ds(tau_of(r, e), 1), :] for e in range(4)], axis=0)
        lsc[q, r, :256] = scaled.astype(jnp.bfloat16)
        lsc[q, r, 256:] = (swap_halves(scaled) * plus_minus).astype(jnp.bfloat16)

    def left_round(r, carry):
        left_rows(0, r)
        left_rows(1, r)
        return carry

    lax.fori_loop(0, 4, left_round, 0, unroll=True)
    grelay(0, 3)
    grelay(0, 2)

    def screen(q, n, r):
        cols = pl.ds(pl.multiple_of(n * 256, 256), 256)
        tile = xs[1 + q, pl.ds(n * 4, 4)].reshape(256, width)
        green = lax.dot_general(lsc[q, r], tile, NT, preferred_element_type=jnp.float32)
        for e in range(4):
            t = tau_of(r, e)
            real_rows, imag_rows = slice(e * 64, e * 64 + 64), slice(256 + e * 64, 320 + e * 64)
            gr, gi = green[real_rows], green[imag_rows]
            wr = wv[q, 0, t, :, cols].astype(jnp.float32)
            wi = wv[q, 1, t, :, cols].astype(jnp.float32)
            sr = gr * wr - gi * wi
            si = gr * wi + gi * wr
            if q == 1:
                sr = sr + scr[r, real_rows, cols].astype(jnp.float32)
                si = si + scr[r, imag_rows, cols].astype(jnp.float32)
            scr[r, real_rows, cols] = sr.astype(jnp.bfloat16)
            scr[r, imag_rows, cols] = si.astype(jnp.bfloat16)

    def tile(q, d):
        n = wrap(z + d)

        def one_round(r, carry):
            screen(q, n, r)
            return carry

        lax.fori_loop(0, 4, one_round, 0, unroll=True)

    gstart_z(2)
    grelay(1, 0)
    gforward(1, 1)
    gforward(1, 3)
    grelay(2, 0)
    gforward(1, 2)
    for i in range(2):
        pltpu.make_async_copy(w_hbm.at[0, i], wv.at[0, i], wsem.at[i]).wait()
    gfinish(1, 0)
    tile(0, 0)
    grelay(1, 1)
    grelay(1, 3)
    gforward(2, 1)
    gforward(2, 3)
    grelay(1, 2)
    gforward(2, 2)
    for i in range(2):
        pltpu.make_async_copy(w_hbm.at[1, i], wv.at[1, i], wsem.at[2 + i]).wait()
    gfinish(2, 0)
    tile(1, 0)
    gfinish(1, 1)
    grelay(2, 1)
    tile(0, 1)
    grelay(2, 3)
    gfinish(1, 3)
    tile(0, 3)
    grelay(2, 2)
    gfinish(1, 2)
    tile(0, 2)
    gfinish(2, 1)
    tile(1, 1)
    gfinish(2, 3)
    tile(1, 3)
    gfinish(2, 2)
    for d in (1, 3, 2):
        gfinish(0, d)

    def hcopy(r, e):
        return pltpu.make_async_remote_copy(
            src_ref=hsend.at[r, e], dst_ref=hrecv.at[r, x], send_sem=hss.at[0],
            recv_sem=hrs.at[r], device_id=(g, wdev(z, wrap(x + e))), device_id_type=MESH)

    def last(r, carry):
        screen(1, wrap(z + 2), r)
        both = lax.dot_general(scr[r], xs[0].reshape(16 * rows, width), NN,
                               preferred_element_type=jnp.float32)
        half = both[:256] + swap_halves(both[256:]) * minus_plus
        half = half.astype(jnp.bfloat16)
        for e in (2, 1, 3):
            hsend[r, e] = half[e * 64:e * 64 + 64]
        hrecv[r, x] = half[:64]
        for e in (2, 1, 3):
            hcopy(r, e).start()
        return carry

    lax.fori_loop(0, 4, last, 0, unroll=True)

    def rcopy(r, d):
        other = wrap(z + d)
        return pltpu.make_async_remote_copy(
            src_ref=rsend.at[r, other], dst_ref=rrecv.at[r, d - 1], send_sem=rss.at[0],
            recv_sem=rrs.at[r // 2], device_id=(g, wdev(other, x)), device_id_type=MESH)

    def project(r):
        pltpu.make_async_remote_copy(
            src_ref=hrecv.at[r, pl.ds(0, 3)], dst_ref=hrecv.at[r, pl.ds(0, 3)], send_sem=hss.at[0],
            recv_sem=hrs.at[r], device_id=(g, right), device_id_type=MESH).wait_recv()
        total = lax.dot_general(xkt[...], hrecv[r].reshape(4 * rows, width), NN,
                                preferred_element_type=jnp.float32)
        sigma = total[:192] + swap_halves(total[192:]) * plus_minus
        sigma = sigma.reshape(4, 48, width)
        rsend[r] = sigma.astype(jnp.bfloat16)
        for d in (2, 1, 3):
            rcopy(r, d).start()

    project(0)
    project(1)
    project(2)
    project(3)

    for part in range(2):
        pltpu.make_async_remote_copy(
            src_ref=rrecv.at[pl.ds(2 * part, 2)], dst_ref=rrecv.at[pl.ds(2 * part, 2)], send_sem=rss.at[0],
            recv_sem=rrs.at[part], device_id=(g, right), device_id_type=MESH).wait_recv()
        sums = []
        for r in (2 * part, 2 * part + 1):
            total = rsend[r, z].astype(jnp.float32)
            for i in range(3):
                total = total + rrecv[r, i].astype(jnp.float32)
            sums.append(total)
        summed = jnp.concatenate(sums, axis=0).astype(jnp.bfloat16)
        pieces = lax.dot_general(order[...], summed, NN, preferred_element_type=jnp.float32)
        fsend[part] = pieces.reshape(4, 24, width).astype(jnp.bfloat16)
        frecv[part, x] = fsend[part, x]
        for e in (2, 1, 3):
            other = wrap(x + e)
            pltpu.make_async_remote_copy(
                src_ref=fsend.at[part, other], dst_ref=frecv.at[part, x], send_sem=fss.at[0],
                recv_sem=frs.at[0], device_id=(g, wdev(z, other)), device_id_type=MESH).start()

    for s in range(3):
        pltpu.make_async_remote_copy(
            src_ref=xs.at[s, pl.ds(0, 15)], dst_ref=xs.at[s, pl.ds(0, 15)], send_sem=gsend.at[s],
            recv_sem=grecv.at[s, 0], device_id=(g, right), device_id_type=MESH).wait_send()
    pltpu.make_async_remote_copy(
        src_ref=kg.at[pl.ds(0, 15)], dst_ref=kg.at[pl.ds(0, 15)], send_sem=ksend.at[0],
        recv_sem=kcore.at[0], device_id=(partner, w), device_id_type=MESH).wait_send()
    pltpu.make_async_remote_copy(
        src_ref=hsend.at[pl.ds(0, 3)], dst_ref=hrecv.at[pl.ds(0, 3)], send_sem=hss.at[0],
        recv_sem=hrs.at[0], device_id=(g, right), device_id_type=MESH).wait_send()
    pltpu.make_async_remote_copy(
        src_ref=rrecv, dst_ref=rrecv, send_sem=rss.at[0],
        recv_sem=rrs.at[0], device_id=(g, right), device_id_type=MESH).wait_send()
    pltpu.make_async_remote_copy(
        src_ref=fwait, dst_ref=fwait, send_sem=fss.at[0],
        recv_sem=frs.at[0], device_id=(g, right), device_id_type=MESH).wait()
    rows_in = frecv[...].astype(jnp.float32).reshape(192, width).astype(jnp.bfloat16)
    result = lax.dot_general(unorder[...], rows_in, NN,
                             preferred_element_type=jnp.float32)
    out_ref[0] = unpack_columns(result).reshape(12, 16, width)


def shards(orbitals, energies, perm_table, momenta, screened_w):
    _, rows, width = orbitals.shape
    taus, points = screened_w.shape[2], screened_w.shape[4]
    bf16, f32 = jnp.bfloat16, jnp.float32
    dma = pltpu.SemaphoreType.DMA
    hbm = pl.BlockSpec(memory_space=pltpu.HBM)
    vmem = pl.BlockSpec(memory_space=pltpu.VMEM)
    sigma = pl.pallas_call(
        kernel,
        out_shape=jax.ShapeDtypeStruct((1, 12, taus, width), f32),
        in_specs=[hbm] * 5,
        out_specs=vmem,
        scratch_shapes=[
            pltpu.VMEM(perm_table.shape[::-1], jnp.int32),
            pltpu.SMEM(momenta.shape, jnp.int32),
            pltpu.VMEM(energies.shape, f32),
            pltpu.VMEM((rows, width), bf16),
            pltpu.VMEM((3, 16, rows, width), bf16),
            pltpu.VMEM((16, rows, width), bf16),
            pltpu.VMEM((2, 2, taus, rows, points), bf16),
            pltpu.VMEM((4, 512, points), bf16),
            pltpu.VMEM((2, 4, 512, width), bf16),
            pltpu.VMEM((4, 4, rows, width), bf16),
            pltpu.VMEM((4, 4, rows, width), bf16),
            pltpu.VMEM((width, 4 * rows), bf16),
            pltpu.VMEM((96, 96), bf16),
            pltpu.VMEM((192, 192), bf16),
            pltpu.VMEM((2, taus, width), f32),
            pltpu.VMEM((4, 4, 48, width), bf16),
            pltpu.VMEM((4, 3, 48, width), bf16),
            pltpu.VMEM((2, 4, 24, width), bf16),
            pltpu.VMEM((2, 4, 24, width), bf16),
            pltpu.VMEM((6, 24, width), bf16),
            dma((3,)), dma((3, 16)), dma((1,)), dma((16,)), dma((1,)),
            dma((1,)), dma((4,)), dma((1,)), dma((2,)), dma((1,)), dma((1,)),
            dma((4,)), dma((4,)),
        ],
        compiler_params=pltpu.CompilerParams(collective_id=0, has_side_effects=True, vmem_limit_bytes=40 * 2**20),
    )(*[pltpu.with_memory_space_constraint(a, pltpu.HBM)
        for a in (perm_table.T, momenta, energies, orbitals, screened_w)])
    return sigma.transpose(0, 2, 1, 3)


def solution(mesh):
    return jax.shard_map(
        shards,
        mesh=mesh,
        in_specs=(P("kgrp", "wrow", None), P(), P(), P(), P(None, None, None, "wrow", None)),
        out_specs=P("kgrp", None, "wrow", None),
        check_vma=False,
    )
```

```python
import functools

import jax
import jax.numpy as jnp
from jax import lax
from jax.experimental import pallas as pl
from jax.experimental.pallas import tpu as pltpu
from jax.sharding import PartitionSpec as P

BETA = 8.0
MESH = pl.DeviceIdType.MESH
NT = (((1,), (1,)), ((), ()))
NN = (((1,), (0,)), ((), ()))


def sign_row(width, first, second):
    half = width // 2
    lane = lax.broadcasted_iota(jnp.int32, (1, width), 1)
    return jnp.where(lane < half, first, second).astype(jnp.float32)


def pack_columns(x):
    return jnp.concatenate([x[:, :192], x[:, 320:], x[:, 192:320]], axis=1)


def unpack_columns(x):
    return jnp.concatenate([x[:, :192], x[:, 256:], x[:, 192:256]], axis=1)


def swap_halves(x):
    return jnp.concatenate([x[:, 256:], pltpu.roll(x[:, 128:256], 64, axis=1), x[:, :128]], axis=1)


def kernel(perm_hbm, mom_hbm, energy_hbm, orb_ref, w_hbm, out_ref,
           perm_ref, mom_ref, energy_ref, own, xs, kg, wv, scr, lsc, hsend, hrecv, xkt, order, unorder, occ,
           rsend, rrecv, fsend, frecv, fwait,
           gsend, grecv, ksend, krecv, kcore, hss, hrs, rss, rrs, fss, frs, wsem, osem):
    g = lax.axis_index("kgrp")
    w = lax.axis_index("wrow")
    y, h, c = lax.div(g, 4), lax.rem(lax.div(g, 2), 2), lax.rem(g, 2)
    z, x = lax.div(w, 4), lax.rem(w, 4)
    rows, width = xs.shape[2], xs.shape[3]
    taus = wv.shape[2]

    def wrap(v):
        return lax.rem(v, 4)

    def kdev(y_, h_, c_):
        return y_ * 4 + h_ * 2 + c_

    def wdev(z_, x_):
        return z_ * 4 + x_

    own_rows = pltpu.make_async_copy(orb_ref.at[0], own, osem.at[0])
    tables = [
        pltpu.make_async_copy(src, dst, osem.at[1 + i])
        for i, (src, dst) in enumerate(((perm_hbm, perm_ref), (mom_hbm, mom_ref), (energy_hbm, energy_ref)))]
    own_rows.start()
    for table in tables:
        table.start()

    barrier = pltpu.get_barrier_semaphore()
    partner = kdev(y, h, 1 - c)
    across = kdev(y, 1 - h, c)
    up, down = kdev(wrap(y + 1), h, c), kdev(wrap(y + 3), h, c)
    beyond = kdev(wrap(y + 2), h, c)
    for peer in (across, up, down, beyond, partner):
        pl.semaphore_signal(barrier, inc=1, device_id=(peer, w), device_id_type=MESH)
    for d in (2, 1, 3):
        pl.semaphore_signal(barrier, inc=1, device_id=(g, wdev(wrap(z + d), x)), device_id_type=MESH)
        pl.semaphore_signal(barrier, inc=1, device_id=(g, wdev(z, wrap(x + d))), device_id_type=MESH)
    own_rows.wait()
    packed = pack_columns(own[...])
    xs[0, w] = packed
    kg[g] = packed
    pl.semaphore_wait(barrier, 11)

    def kcopy(block, peer):
        return pltpu.make_async_remote_copy(
            src_ref=kg.at[block], dst_ref=kg.at[block], send_sem=ksend.at[0],
            recv_sem=krecv.at[block], device_id=(peer, w), device_id_type=MESH)

    def kpass(block):
        pltpu.make_async_remote_copy(
            src_ref=kg.at[block], dst_ref=kg.at[block], send_sem=ksend.at[0],
            recv_sem=kcore.at[0], device_id=(partner, w), device_id_type=MESH).start()

    def kwait(block):
        kcopy(block, across).wait_recv()

    def gcopy(s, block, peer):
        return pltpu.make_async_remote_copy(
            src_ref=xs.at[s, block], dst_ref=xs.at[s, block], send_sem=gsend.at[s],
            recv_sem=grecv.at[s, block], device_id=(g, peer), device_id_type=MESH)

    left, right = wdev(z, wrap(x + 3)), wdev(z, wrap(x + 1))

    def gwait(s, block):
        gcopy(s, block, right).wait_recv()

    def gstart_z(s):
        gcopy(s, w, wdev(wrap(z + 1), x)).start()
        gcopy(s, w, wdev(wrap(z + 3), x)).start()
        gcopy(s, w, wdev(wrap(z + 2), x)).start()

    def gstart_x(s):
        gcopy(s, w, right).start()
        gcopy(s, w, left).start()

    def gforward(s, d):
        block = wdev(wrap(z + d), x)
        gwait(s, block)
        gcopy(s, block, right).start()
        gcopy(s, block, left).start()

    def grelay(s, d):
        if d < 2:
            block, peer = wdev(wrap(z + d), wrap(x + 3)), right
        else:
            block, peer = wdev(wrap(z + d), wrap(x + 1)), left
        gwait(s, block)
        gcopy(s, block, peer).start()

    def gfinish(s, d):
        gwait(s, wdev(wrap(z + d), wrap(x + (1 if d < 2 else 3))))
        gwait(s, wdev(wrap(z + d), wrap(x + 2)))

    def kspread(block):
        for peer in (beyond, up, down):
            kcopy(block, peer).start()

    def ktake(yy, hh):
        block = kdev(wrap(y + yy), hh, c)
        kwait(block)
        kpass(block)

    kcopy(g, across).start()
    kspread(g)
    gstart_x(0)
    kpass(g)
    for i in range(4):
        pltpu.make_async_copy(w_hbm.at[i // 2, i % 2], wv.at[i // 2, i % 2], wsem.at[i]).start()
    ktake(1, h)
    gstart_z(0)
    ktake(3, h)
    ktake(2, h)
    grelay(0, 0)
    row = lax.broadcasted_iota(jnp.int32, (96, 96), 0)
    col = lax.broadcasted_iota(jnp.int32, (96, 96), 1)
    part, inner = lax.div(row, 24), lax.rem(row, 24)
    split = lax.div(inner, 12) * 48 + part * 12 + lax.rem(inner, 12)
    order[...] = jnp.where(col == split, 1.0, 0.0).astype(jnp.bfloat16)
    row = lax.broadcasted_iota(jnp.int32, (192, 192), 0)
    col = lax.broadcasted_iota(jnp.int32, (192, 192), 1)
    tau_row = lax.rem(row, 16)
    late, odd = lax.div(tau_row, 8), lax.rem(lax.div(tau_row, 4), 2)
    merge = late * 96 + lax.rem(tau_row, 4) * 24 + odd * 12 + lax.div(row, 16)
    unorder[...] = jnp.where(col == merge, 1.0, 0.0).astype(jnp.bfloat16)
    for table in tables:
        table.wait()
    own_row = perm_ref[pl.ds(g, 1), :]
    lane = lax.broadcasted_iota(jnp.int32, own_row.shape, 1)
    sources = [jnp.sum(jnp.where(lane == mom_ref[q], own_row, 0)) for q in range(2)]
    mine = kdev(y, 1 - h, c)
    kwait(mine)
    kspread(mine)
    kpass(mine)
    gforward(0, 1)
    gforward(0, 3)
    gforward(0, 2)
    ktake(1, 1 - h)
    ktake(3, 1 - h)
    ktake(2, 1 - h)
    gfinish(0, 0)
    row = lax.broadcasted_iota(jnp.int32, (width, width), 0)
    col = lax.broadcasted_iota(jnp.int32, (width, width), 1)
    want = jnp.where(row < 192, row, 192 + lax.rem(row + 64, 192))
    pick = jnp.where(want == col, 1.0, 0.0).astype(jnp.bfloat16)
    strip = xs[0, pl.ds(z * 4, 4)].reshape(4 * rows, width)
    xkt[...] = lax.dot_general(pick, strip, NT, preferred_element_type=jnp.float32).astype(jnp.bfloat16)
    grelay(0, 1)
    pltpu.make_async_remote_copy(
        src_ref=kg.at[pl.ds(0, 8)], dst_ref=kg.at[pl.ds(0, 8)], send_sem=ksend.at[0],
        recv_sem=kcore.at[0], device_id=(partner, w), device_id_type=MESH).wait_recv()

    for q in range(2):
        xs[1 + q, w] = kg[sources[q]]
    gstart_z(1)
    gstart_x(1)
    gstart_x(2)

    minus_plus = sign_row(width, -1.0, 1.0)
    plus_minus = sign_row(width, 1.0, -1.0)
    tau = (lax.broadcasted_iota(jnp.int32, (taus, 1), 0).astype(jnp.float32) + 0.5) * (BETA / taus)
    for q in range(2):
        energy = energy_ref[pl.ds(sources[q], 1), :]
        soft = -BETA * energy
        soft = jnp.maximum(soft, 0.0) + jnp.log(1.0 + jnp.exp(-jnp.abs(soft)))
        factor = -jnp.exp(-tau * energy - soft)
        occ[q] = pack_columns(jnp.concatenate([factor, factor], axis=1))

    def tau_of(r, e):
        return r * 4 + wrap(x + e)

    def left_rows(q, r):
        base = xs[1 + q, w].astype(jnp.float32)
        scaled = jnp.concatenate(
            [base * occ[q, pl.ds(tau_of(r, e), 1), :] for e in range(4)], axis=0)
        lsc[q, r, :256] = scaled.astype(jnp.bfloat16)
        lsc[q, r, 256:] = (swap_halves(scaled) * plus_minus).astype(jnp.bfloat16)

    def left_round(r, carry):
        left_rows(0, r)
        left_rows(1, r)
        return carry

    lax.fori_loop(0, 4, left_round, 0, unroll=True)
    grelay(0, 3)
    grelay(0, 2)

    def screen(q, n, r):
        cols = pl.ds(pl.multiple_of(n * 256, 256), 256)
        tile = xs[1 + q, pl.ds(n * 4, 4)].reshape(256, width)
        green = lax.dot_general(lsc[q, r], tile, NT, preferred_element_type=jnp.float32)
        for e in range(4):
            t = tau_of(r, e)
            real_rows, imag_rows = slice(e * 64, e * 64 + 64), slice(256 + e * 64, 320 + e * 64)
            gr, gi = green[real_rows], green[imag_rows]
            wr = wv[q, 0, t, :, cols].astype(jnp.float32)
            wi = wv[q, 1, t, :, cols].astype(jnp.float32)
            sr = gr * wr - gi * wi
            si = gr * wi + gi * wr
            if q == 1:
                sr = sr + scr[r, real_rows, cols].astype(jnp.float32)
                si = si + scr[r, imag_rows, cols].astype(jnp.float32)
            scr[r, real_rows, cols] = sr.astype(jnp.bfloat16)
            scr[r, imag_rows, cols] = si.astype(jnp.bfloat16)

    def tile(q, d):
        n = wrap(z + d)

        def one_round(r, carry):
            screen(q, n, r)
            return carry

        lax.fori_loop(0, 4, one_round, 0, unroll=True)

    gstart_z(2)
    grelay(1, 0)
    gforward(1, 1)
    gforward(1, 3)
    grelay(2, 0)
    gforward(1, 2)
    for i in range(2):
        pltpu.make_async_copy(w_hbm.at[0, i], wv.at[0, i], wsem.at[i]).wait()
    gfinish(1, 0)
    tile(0, 0)
    grelay(1, 1)
    grelay(1, 3)
    gforward(2, 1)
    gforward(2, 3)
    grelay(1, 2)
    gforward(2, 2)
    for i in range(2):
        pltpu.make_async_copy(w_hbm.at[1, i], wv.at[1, i], wsem.at[2 + i]).wait()
    gfinish(2, 0)
    tile(1, 0)
    gfinish(1, 1)
    grelay(2, 1)
    tile(0, 1)
    grelay(2, 3)
    gfinish(1, 3)
    tile(0, 3)
    grelay(2, 2)
    gfinish(1, 2)
    tile(0, 2)
    gfinish(2, 1)
    tile(1, 1)
    gfinish(2, 3)
    tile(1, 3)
    gfinish(2, 2)
    for d in (1, 3, 2):
        gfinish(0, d)

    def hcopy(r, e):
        return pltpu.make_async_remote_copy(
            src_ref=hsend.at[r, e], dst_ref=hrecv.at[r, x], send_sem=hss.at[0],
            recv_sem=hrs.at[r], device_id=(g, wdev(z, wrap(x + e))), device_id_type=MESH)

    def last(r, carry):
        screen(1, wrap(z + 2), r)
        both = lax.dot_general(scr[r], xs[0].reshape(16 * rows, width), NN,
                               preferred_element_type=jnp.float32)
        half = both[:256] + swap_halves(both[256:]) * minus_plus
        half = half.astype(jnp.bfloat16)
        for e in (2, 1, 3):
            hsend[r, e] = half[e * 64:e * 64 + 64]
        hrecv[r, x] = half[:64]
        for e in (2, 1, 3):
            hcopy(r, e).start()
        return carry

    lax.fori_loop(0, 4, last, 0, unroll=True)

    def rcopy(r, d):
        other = wrap(z + d)
        return pltpu.make_async_remote_copy(
            src_ref=rsend.at[r, other], dst_ref=rrecv.at[r, d - 1], send_sem=rss.at[0],
            recv_sem=rrs.at[r // 2], device_id=(g, wdev(other, x)), device_id_type=MESH)

    def project(r):
        pltpu.make_async_remote_copy(
            src_ref=hrecv.at[r, pl.ds(0, 3)], dst_ref=hrecv.at[r, pl.ds(0, 3)], send_sem=hss.at[0],
            recv_sem=hrs.at[r], device_id=(g, right), device_id_type=MESH).wait_recv()
        total = lax.dot_general(xkt[...], hrecv[r].reshape(4 * rows, width), NN,
                                preferred_element_type=jnp.float32)
        sigma = total[:192] + swap_halves(total[192:]) * plus_minus
        sigma = sigma.reshape(4, 48, width)
        rsend[r] = sigma.astype(jnp.bfloat16)
        for d in (2, 1, 3):
            rcopy(r, d).start()

    project(0)
    project(1)
    project(2)
    project(3)

    for part in range(2):
        pltpu.make_async_remote_copy(
            src_ref=rrecv.at[pl.ds(2 * part, 2)], dst_ref=rrecv.at[pl.ds(2 * part, 2)], send_sem=rss.at[0],
            recv_sem=rrs.at[part], device_id=(g, right), device_id_type=MESH).wait_recv()
        sums = []
        for r in (2 * part, 2 * part + 1):
            total = rsend[r, z].astype(jnp.float32)
            for i in range(3):
                total = total + rrecv[r, i].astype(jnp.float32)
            sums.append(total)
        summed = jnp.concatenate(sums, axis=0).astype(jnp.bfloat16)
        pieces = lax.dot_general(order[...], summed, NN, preferred_element_type=jnp.float32)
        fsend[part] = pieces.reshape(4, 24, width).astype(jnp.bfloat16)
        frecv[part, x] = fsend[part, x]
        for e in (2, 1, 3):
            other = wrap(x + e)
            pltpu.make_async_remote_copy(
                src_ref=fsend.at[part, other], dst_ref=frecv.at[part, x], send_sem=fss.at[0],
                recv_sem=frs.at[0], device_id=(g, wdev(z, other)), device_id_type=MESH).start()

    for s in range(3):
        pltpu.make_async_remote_copy(
            src_ref=xs.at[s, pl.ds(0, 15)], dst_ref=xs.at[s, pl.ds(0, 15)], send_sem=gsend.at[s],
            recv_sem=grecv.at[s, 0], device_id=(g, right), device_id_type=MESH).wait_send()
    pltpu.make_async_remote_copy(
        src_ref=kg.at[pl.ds(0, 15)], dst_ref=kg.at[pl.ds(0, 15)], send_sem=ksend.at[0],
        recv_sem=kcore.at[0], device_id=(partner, w), device_id_type=MESH).wait_send()
    pltpu.make_async_remote_copy(
        src_ref=hsend.at[pl.ds(0, 3)], dst_ref=hrecv.at[pl.ds(0, 3)], send_sem=hss.at[0],
        recv_sem=hrs.at[0], device_id=(g, right), device_id_type=MESH).wait_send()
    pltpu.make_async_remote_copy(
        src_ref=rrecv, dst_ref=rrecv, send_sem=rss.at[0],
        recv_sem=rrs.at[0], device_id=(g, right), device_id_type=MESH).wait_send()
    pltpu.make_async_remote_copy(
        src_ref=fwait, dst_ref=fwait, send_sem=fss.at[0],
        recv_sem=frs.at[0], device_id=(g, right), device_id_type=MESH).wait()
    rows_in = frecv[...].astype(jnp.float32).reshape(192, width).astype(jnp.bfloat16)
    result = lax.dot_general(unorder[...], rows_in, NN,
                             preferred_element_type=jnp.float32)
    out_ref[0] = unpack_columns(result).reshape(12, 16, width)


def shards(orbitals, energies, perm_table, momenta, screened_w):
    _, rows, width = orbitals.shape
    taus, points = screened_w.shape[2], screened_w.shape[4]
    bf16, f32 = jnp.bfloat16, jnp.float32
    dma = pltpu.SemaphoreType.DMA
    hbm = pl.BlockSpec(memory_space=pltpu.HBM)
    vmem = pl.BlockSpec(memory_space=pltpu.VMEM)
    sigma = pl.pallas_call(
        kernel,
        out_shape=jax.ShapeDtypeStruct((1, 12, taus, width), f32),
        in_specs=[hbm] * 5,
        out_specs=vmem,
        scratch_shapes=[
            pltpu.VMEM(perm_table.shape[::-1], jnp.int32),
            pltpu.SMEM(momenta.shape, jnp.int32),
            pltpu.VMEM(energies.shape, f32),
            pltpu.VMEM((rows, width), bf16),
            pltpu.VMEM((3, 16, rows, width), bf16),
            pltpu.VMEM((16, rows, width), bf16),
            pltpu.VMEM((2, 2, taus, rows, points), bf16),
            pltpu.VMEM((4, 512, points), bf16),
            pltpu.VMEM((2, 4, 512, width), bf16),
            pltpu.VMEM((4, 4, rows, width), bf16),
            pltpu.VMEM((4, 4, rows, width), bf16),
            pltpu.VMEM((width, 4 * rows), bf16),
            pltpu.VMEM((96, 96), bf16),
            pltpu.VMEM((192, 192), bf16),
            pltpu.VMEM((2, taus, width), f32),
            pltpu.VMEM((4, 4, 48, width), bf16),
            pltpu.VMEM((4, 3, 48, width), bf16),
            pltpu.VMEM((2, 4, 24, width), bf16),
            pltpu.VMEM((2, 4, 24, width), bf16),
            pltpu.VMEM((6, 24, width), bf16),
            dma((3,)), dma((3, 16)), dma((1,)), dma((16,)), dma((1,)),
            dma((1,)), dma((4,)), dma((1,)), dma((2,)), dma((1,)), dma((1,)),
            dma((4,)), dma((4,)),
        ],
        compiler_params=pltpu.CompilerParams(collective_id=0, has_side_effects=True, vmem_limit_bytes=40 * 2**20),
    )(*[pltpu.with_memory_space_constraint(a, pltpu.HBM)
        for a in (perm_table.T, momenta, energies, orbitals, screened_w)])
    return sigma.transpose(0, 2, 1, 3)


def solution(mesh):
    return jax.shard_map(
        shards,
        mesh=mesh,
        in_specs=(P("kgrp", "wrow", None), P(), P(), P(), P(None, None, None, "wrow", None)),
        out_specs=P("kgrp", None, "wrow", None),
        check_vma=False,
    )
```
